32 devices in a mesh: batch: 8 (over z, y), space: 4 (over x, core).
Axes of the slice: x: 2, y: 2, z: 4, core: 2. Of those that a mesh axis runs over, the one named last changes fastest.
Arguments:
- volume: bfloat16 [16, 32, 16, 1024], P('batch', None, 'space'), may hold values from -6 to 6
- conv_one: bfloat16 [3, 3, 3, 32, 32], replicated, may hold values from -0.21875 to 0.21875
- conv_two: bfloat16 [3, 3, 3, 32, 32], replicated, may hold values from -0.21875 to 0.21875
- conv_three: bfloat16 [3, 3, 3, 64, 32], replicated, may hold values from -0.21875 to 0.21875
- dense_weight: bfloat16 [2048, 128], P('batch'), may hold values from -0.125 to 0.125
Outputs:
- dense_out: float32 [16, 128], P('batch')
The draws below stay inside these ranges and needn't reach their ends.
All inputs are finite; a program needn't handle non-finite values.
Results may differ from the reference program's by a relative error of at most 0.01.
Values may be sent and summed in bfloat16 or wider, within the bound.
A program may use at most 64 MiB of HBM per device.

```python
import jax
import jax.numpy as jnp
from jax import lax

C1 = 32
C2 = 64
HID = 128
NXY = 32
NZ = 16
SAMPLES = 16
FEAT = 2048


def block_scale(rng, extent, split, smallest, largest):
    def one(axis_at, shards_of):
        heights = jax.random.uniform(jax.random.fold_in(jax.random.fold_in(rng, 6), axis_at), (shards_of,), jnp.float32, smallest / len(split), largest / len(split))
        return jnp.repeat(jnp.exp(heights), extent[axis_at] // shards_of).reshape((-1,) + (1,) * (len(extent) - axis_at - 1))

    loudness = one(*split[0])
    for cut in split[1:]:
        loudness = loudness * one(*cut)
    return loudness


def scatter_about(own_key, dims, width, most, cuts=(), dtype=jnp.bfloat16):
    factor_of = block_scale(own_key, dims, cuts, -0.22, 0.18) if cuts else 1.0
    array = jax.random.normal(own_key, dims, jnp.float32) * width * factor_of
    return jnp.minimum(jnp.maximum(array, -most), most).astype(dtype)


def setup_inputs(seed: int = 0) -> dict:
    keys = jax.random.split(jax.random.key(seed), 6)
    return {
        "volume": scatter_about(keys[0], (SAMPLES, C1, NZ, NXY * NXY), 1.0, 6.0, ((0, 8), (2, 4))),
        "conv_one": scatter_about(keys[1], (3, 3, 3, C1, C1), (27 * C1) ** -0.5, 0.21875),
        "conv_two": scatter_about(keys[2], (3, 3, 3, C1, C1), (27 * C1) ** -0.5, 0.21875),
        "conv_three": scatter_about(keys[3], (3, 3, 3, C2, C1), (27 * C1) ** -0.5, 0.21875),
        "dense_weight": scatter_about(keys[4], (FEAT, HID), FEAT ** -0.5, 0.125, ((0, 8),)),
    }


def activate(values):
    return jnp.where(values > 0, values, 0.3 * values)


def conv_cube(cube, weight):
    data = cube.astype(jnp.float32)
    kernel = weight.astype(jnp.float32)
    summed = jnp.zeros((weight.shape[3],) + cube.shape[1:], jnp.float32)
    for depth_idx in range(3):
        for row_idx in range(3):
            for col_idx in range(3):
                moved = jnp.roll(data, (1 - depth_idx, 1 - row_idx, 1 - col_idx), axis=(1, 2, 3))
                summed = summed + jnp.einsum("oc,czyx->ozyx", kernel[depth_idx, row_idx, col_idx], moved)
    return summed


def pool_cube(cube):
    chans, depth, rows, cols = cube.shape
    blocks = cube.reshape(chans, depth // 2, 2, rows // 2, 2, cols // 2, 2)
    return jnp.max(blocks, axis=(2, 4, 6))


def reference(volume, conv_one, conv_two, conv_three, dense_weight):
    def per_sample(sample):
        cube = sample.reshape(C1, NZ, NXY, NXY)
        hidden_one = activate(conv_cube(cube, conv_one)).astype(jnp.bfloat16)
        hidden_two = activate(conv_cube(hidden_one, conv_two)).astype(jnp.bfloat16)
        pooled = pool_cube(hidden_two)
        third = activate(conv_cube(pooled, conv_three))
        final = pool_cube(pool_cube(third)).astype(jnp.bfloat16)
        return jnp.transpose(final, (1, 0, 2, 3)).reshape(-1)

    features = lax.map(per_sample, volume)
    return jnp.dot(features, dense_weight, preferred_element_type=jnp.float32)
```

```python
import functools

import jax
import jax.numpy as jnp
from jax import lax
from jax.experimental import pallas as pl
from jax.experimental.pallas import tpu as pltpu
from jax.sharding import PartitionSpec as P

NXY = 32
C1 = 32
BF = jnp.bfloat16
F32 = jnp.float32
MESH = pl.DeviceIdType.MESH


def activate(values):
    return jnp.where(values > 0, values, 0.3 * values)


def dot(lhs, rhs):
    return jnp.dot(lhs, rhs, preferred_element_type=F32)


def ahead(values, off):
    return pltpu.roll(values, (-off) % values.shape[1], 1)


def put_taps(values, dst, base, extent):
    rows = values.shape[0]
    column = lax.broadcasted_iota(jnp.int32, values.shape, 1) % extent
    for col_idx in range(3):
        off = col_idx - 1
        moved = values
        if off:
            border = extent - 1 if off == 1 else 0
            moved = jnp.where(
                column == border, ahead(values, off - off * extent), ahead(values, off)
            )
        for row_idx in range(3):
            tap = row_idx * 3 + col_idx
            turned = ahead(moved, (row_idx - 1) * extent) if row_idx != 1 else moved
            dst[base + tap * rows : base + (tap + 1) * rows, :] = turned


def lay_weights(w_ref, own, low, high, outs):
    spread = (
        lax.broadcasted_iota(jnp.int32, (C1, 128), 1) % C1
        == lax.broadcasted_iota(jnp.int32, (C1, 128), 0)
    )
    spread = jnp.where(spread, 1.0, 0.0).astype(BF)
    wide = dot(w_ref[...], spread)
    group = lax.broadcasted_iota(jnp.int32, (outs, 128), 1) // C1

    def piece(depth, tap):
        at = (depth * 9 + tap) * outs
        return wide[at : at + outs, :]

    for tap in range(9):
        for plane in range(4):
            block = jnp.zeros((outs, 128), F32)
            for depth in range(3):
                block = jnp.where(group == plane + depth - 1, piece(depth, tap), block)
            own[plane * outs : (plane + 1) * outs, tap * 128 : (tap + 1) * 128] = block.astype(BF)
    for dst, depth in ((low, 0), (high, 2)):
        for part in range(3):
            block = jnp.zeros((outs, 128), F32)
            for lane in range(4):
                if part * 4 + lane < 9:
                    block = jnp.where(group == lane, piece(depth, part * 4 + lane), block)
            dst[:, part * 128 : (part + 1) * 128] = block.astype(BF)


def kernel(
    count, batches, vol_ref, w1_ref, w2_ref, w3_ref, dw_ref, out_ref,
    own1, low1, high1, own2, low2, high2, own3, low3, high3,
    x_ref, vh, h1, hh, xcol, hcol, acc, sent, slab, edge, xcol3, hcol3, wd, fin,
    v_send, v_recv, h_send, h_recv, p_send, p_recv, e_send, e_recv,
    w_send, w_recv, f_send, f_recv,
):
    me = lax.axis_index("space")
    lot = lax.axis_index("batch")
    parity = lax.rem(me, 2)
    block = me // 2
    blocks = count // 2
    right = lax.rem(me + 1, count)
    left = lax.rem(me + count - 1, count)
    shards = batches // blocks

    barrier = pltpu.get_barrier_semaphore()
    for step in range(1, count):
        pl.semaphore_signal(
            barrier, inc=1, device_id={"space": lax.rem(me + step, count)}, device_id_type=MESH
        )
    for step in range(1, batches):
        pl.semaphore_signal(
            barrier, inc=1, device_id={"batch": lax.rem(lot + step, batches)}, device_id_type=MESH
        )
    for sample in range(2):
        for plane in range(4):
            x_ref[sample, plane * C1 : (plane + 1) * C1, :] = vol_ref[sample, :, plane, :]
    pl.semaphore_wait(barrier, count + batches - 2)

    def halo_copies(src, dst, send, recv, sample):
        up = pltpu.make_async_remote_copy(
            src_ref=src.at[sample, 96:128], dst_ref=dst.at[sample, 0],
            send_sem=send.at[sample, 0], recv_sem=recv.at[sample, 0],
            device_id={"space": right}, device_id_type=MESH,
        )
        down = pltpu.make_async_remote_copy(
            src_ref=src.at[sample, 0:32], dst_ref=dst.at[sample, 1],
            send_sem=send.at[sample, 1], recv_sem=recv.at[sample, 1],
            device_id={"space": left}, device_id_type=MESH,
        )
        return up, down

    order = (parity, 1 - parity)
    v_copies = [halo_copies(x_ref, vh, v_send, v_recv, sample) for sample in order]
    for pair in v_copies:
        for copy in pair:
            copy.start()

    def row_copy(step):
        target = lax.rem(lot + step, batches)
        return pltpu.make_async_remote_copy(
            src_ref=dw_ref, dst_ref=wd.at[lax.rem(lot, shards)],
            send_sem=w_send.at[step], recv_sem=w_recv.at[lax.rem(lot, shards)],
            device_id={"batch": target}, device_id_type=MESH,
        )

    gives = lot // shards == block

    @pl.when(gives)
    def _():
        for step in range(1, batches):
            row_copy(step).start()
        wd[lax.rem(lot, shards)] = dw_ref[...]

    lay_weights(w1_ref, own1, low1, high1, C1)

    def own_part(values, weight, sample):
        put_taps(values, xcol, 0, NXY)
        for part in range(4):
            cols = slice(part * 256, (part + 1) * 256)
            acc[sample, :, cols] = dot(weight[...], xcol[:, cols])

    def halo_part(halo, low, high, sample):
        put_taps(halo[sample, 0], hcol, 0, NXY)
        put_taps(halo[sample, 1], hcol, 288, NXY)
        for part in range(4):
            cols = slice(part * 256, (part + 1) * 256)
            acc[sample, 0:32, cols] += dot(low[:, 0:288], hcol[0:288, cols])
            acc[sample, 96:128, cols] += dot(high[:, 0:288], hcol[288:576, cols])

    for sample in order:
        own_part(x_ref[sample], own1, sample)
    h_copies = []
    for sample, pair in zip(order, v_copies):
        for copy in pair:
            copy.wait_recv()
        halo_part(vh, low1, high1, sample)
        h1[sample] = activate(acc[sample]).astype(BF)
        pair = halo_copies(h1, hh, h_send, h_recv, sample)
        for copy in pair:
            copy.start()
        h_copies.append(pair)

    lay_weights(w2_ref, own2, low2, high2, C1)
    lay_weights(w3_ref, own3, low3, high3, 2 * C1)
    half = NXY // 2
    at = lax.broadcasted_iota(jnp.int32, (NXY * NXY, half * half), 0)
    cell = lax.broadcasted_iota(jnp.int32, (NXY * NXY, half * half), 1)
    pick = jnp.where(at == (cell // half) * 2 * NXY + (cell % half) * 2, 1.0, 0.0).astype(BF)

    def pooled_of(sample):
        low = jnp.maximum(acc[sample, 0:32], acc[sample, 32:64])
        high = jnp.maximum(acc[sample, 64:96], acc[sample, 96:128])
        best = jnp.concatenate([low, high], axis=0)
        best = jnp.maximum(best, ahead(best, 1))
        best = jnp.maximum(best, ahead(best, NXY))
        return dot(activate(best).astype(BF), pick).astype(BF)

    def edge_copy(src, owner, slot):
        step = jnp.where(parity == 0, blocks - 1, 1)
        target = lax.rem(block + step, blocks) * 2 + owner
        return pltpu.make_async_remote_copy(
            src_ref=src.at[pl.ds(pl.multiple_of(parity * C1, C1), C1)],
            dst_ref=edge.at[1 - parity],
            send_sem=e_send.at[slot], recv_sem=e_recv.at[1 - parity],
            device_id={"space": target}, device_id_type=MESH,
        )

    partner_copy = pltpu.make_async_remote_copy(
        src_ref=sent, dst_ref=slab.at[parity], send_sem=p_send, recv_sem=p_recv,
        device_id={"space": block * 2 + 1 - parity}, device_id_type=MESH,
    )
    edge_copies = (edge_copy(sent, 1 - parity, 0), edge_copy(slab.at[parity], parity, 1))
    for turn in (1, 0):
        sample = order[turn]
        put = h1[sample]
        own_part(put, own2, sample)
        for copy in h_copies[turn]:
            copy.wait_recv()
        halo_part(hh, low2, high2, sample)
        pooled = pooled_of(sample)
        if turn == 1:
            sent[...] = pooled
            edge_copies[0].start()
            partner_copy.start()
        else:
            slab[parity] = pooled
            edge_copies[1].start()

    spot = lax.broadcasted_iota(jnp.int32, (half * half, 1024), 0)
    feat = lax.broadcasted_iota(jnp.int32, (half * half, 1024), 1) % 16
    pick_last = jnp.where(spot == (feat // 4) * 4 * half + (feat % 4) * 4, 1.0, 0.0).astype(BF)

    partner_copy.wait_recv()
    put_taps(jnp.concatenate([slab[0], slab[1]], axis=0), xcol3, 0, half)
    third = dot(own3[...], xcol3[...])
    for side in range(2):
        pltpu.make_async_remote_copy(
            src_ref=edge.at[side], dst_ref=edge.at[side],
            send_sem=e_send.at[side], recv_sem=e_recv.at[side],
            device_id={"space": right}, device_id_type=MESH,
        ).wait_recv()
    put_taps(edge[0], hcol3, 0, half)
    put_taps(edge[1], hcol3, 288, half)
    outs = 2 * C1
    best = jnp.maximum(
        jnp.maximum(third[outs : 2 * outs], third[2 * outs : 3 * outs]),
        jnp.maximum(
            third[0:outs] + dot(low3[:, 0:288], hcol3[0:288, :]),
            third[3 * outs :] + dot(high3[:, 0:288], hcol3[288:576, :]),
        ),
    )
    for off in (1, 2, half, 2 * half):
        best = jnp.maximum(best, ahead(best, off))
    cells = dot(activate(best).astype(BF), pick_last)
    mine = lax.broadcasted_iota(jnp.int32, cells.shape, 1) // 16
    mine = mine == lax.broadcasted_iota(jnp.int32, cells.shape, 0)
    feats = jnp.sum(jnp.where(mine, cells, 0.0), axis=0, keepdims=True).astype(BF)
    for slot in range(shards):
        @pl.when(block * shards + slot != lot)
        def _():
            pltpu.make_async_remote_copy(
                src_ref=dw_ref, dst_ref=wd.at[slot],
                send_sem=w_send.at[0], recv_sem=w_recv.at[slot],
                device_id={"batch": lax.rem(lot + 1, batches)}, device_id_type=MESH,
            ).wait_recv()
    rows = dw_ref.shape[0]
    total = jnp.zeros((8, 128), F32)
    feats = jnp.broadcast_to(feats.astype(F32), (8, feats.shape[1])).astype(BF)
    for slot in range(shards):
        total += dot(feats[:, slot * rows : (slot + 1) * rows], wd[slot])
    fin[me] = total

    def fin_copy(step):
        return pltpu.make_async_remote_copy(
            src_ref=fin.at[me], dst_ref=fin.at[me],
            send_sem=f_send.at[step], recv_sem=f_recv.at[step],
            device_id={"space": lax.rem(me + step, count)}, device_id_type=MESH,
        )

    fin_copies = [fin_copy(step) for step in range(1, count)]
    for copy in fin_copies:
        copy.start()
    for pair in v_copies + h_copies:
        for copy in pair:
            copy.wait_send()
    for copy in edge_copies:
        copy.wait_send()
    partner_copy.wait_send()

    @pl.when(gives)
    def _():
        for step in range(1, batches):
            row_copy(step).wait_send()

    for copy in fin_copies:
        copy.wait_send()
    for step in range(1, count):
        source = lax.rem(me + count - step, count)
        pltpu.make_async_remote_copy(
            src_ref=fin.at[source], dst_ref=fin.at[source],
            send_sem=f_send.at[step], recv_sem=f_recv.at[step],
            device_id={"space": right}, device_id_type=MESH,
        ).wait_recv()
    for sample in range(2):
        row = fin[sample]
        for other in range(1, blocks):
            row = row + fin[2 * other + sample]
        out_ref[sample : sample + 1, :] = row[0:1, :]


def per_device(count, batches, volume, conv_one, conv_two, conv_three, dense_weight):
    flat = NXY * NXY
    small = flat // 4
    shards = batches // (count // 2)
    vmem, dma = pltpu.VMEM, pltpu.SemaphoreType.DMA
    return pl.pallas_call(
        functools.partial(kernel, count, batches),
        out_shape=jax.ShapeDtypeStruct((2, dense_weight.shape[1]), F32),
        in_specs=[pl.BlockSpec(memory_space=vmem)] * 5,
        out_specs=pl.BlockSpec(memory_space=vmem),
        scratch_shapes=[
            vmem((128, 1152), BF), vmem((32, 384), BF), vmem((32, 384), BF),
            vmem((128, 1152), BF), vmem((32, 384), BF), vmem((32, 384), BF),
            vmem((256, 1152), BF), vmem((64, 384), BF), vmem((64, 384), BF),
            vmem((2, 128, flat), BF),
            vmem((2, 2, 32, flat), BF),
            vmem((2, 128, flat), BF),
            vmem((2, 2, 32, flat), BF),
            vmem((1152, flat), BF),
            vmem((576, flat), BF),
            vmem((2, 128, flat), F32),
            vmem((64, small), BF),
            vmem((2, 64, small), BF),
            vmem((2, 32, small), BF),
            vmem((1152, small), BF),
            vmem((576, small), BF),
            vmem((shards,) + dense_weight.shape, BF),
            vmem((count, 8, 128), F32),
            dma((2, 2)), dma((2, 2)), dma((2, 2)), dma((2, 2)),
            dma, dma, dma((2,)), dma((2,)),
            dma((batches,)), dma((shards,)), dma((count,)), dma((count,)),
        ],
        compiler_params=pltpu.CompilerParams(
            collective_id=0, has_side_effects=True, vmem_limit_bytes=40 << 20
        ),
    )(
        volume,
        conv_one.reshape(-1, C1),
        conv_two.reshape(-1, C1),
        conv_three.reshape(-1, C1),
        dense_weight,
    )


def solution(mesh):
    in_specs = (P("batch", None, "space", None), P(), P(), P(), P("batch", None))
    return jax.shard_map(
        functools.partial(per_device, mesh.shape["space"], mesh.shape["batch"]),
        mesh=mesh,
        in_specs=in_specs,
        out_specs=P("batch", None),
        check_vma=False,
    )
```

```python
import functools

import jax
import jax.numpy as jnp
from jax import lax
from jax.experimental import pallas as pl
from jax.experimental.pallas import tpu as pltpu
from jax.sharding import PartitionSpec as P

NXY = 32
C1 = 32
BF = jnp.bfloat16
F32 = jnp.float32
MESH = pl.DeviceIdType.MESH


def activate(values):
    return jnp.where(values > 0, values, 0.3 * values)


def dot(lhs, rhs):
    return jnp.dot(lhs, rhs, preferred_element_type=F32)


def ahead(values, off):
    return pltpu.roll(values, (-off) % values.shape[1], 1)


def put_taps(values, dst, base, extent):
    rows = values.shape[0]
    column = lax.broadcasted_iota(jnp.int32, values.shape, 1) % extent
    for col_idx in range(3):
        off = col_idx - 1
        moved = values
        if off:
            border = extent - 1 if off == 1 else 0
            moved = jnp.where(
                column == border, ahead(values, off - off * extent), ahead(values, off)
            )
        for row_idx in range(3):
            tap = row_idx * 3 + col_idx
            turned = ahead(moved, (row_idx - 1) * extent) if row_idx != 1 else moved
            dst[base + tap * rows : base + (tap + 1) * rows, :] = turned


def lay_weights(w_ref, own, low, high, outs):
    spread = (
        lax.broadcasted_iota(jnp.int32, (C1, 128), 1) % C1
        == lax.broadcasted_iota(jnp.int32, (C1, 128), 0)
    )
    spread = jnp.where(spread, 1.0, 0.0).astype(BF)
    turned = w_ref.shape[1] != C1
    wide = w_ref[...].T if turned else dot(w_ref[...], spread)
    group = lax.broadcasted_iota(jnp.int32, (outs, 128), 1) // C1

    pieces = []
    for at in range(27):
        if turned:
            pieces.append(dot(wide[:, at * C1 : (at + 1) * C1], spread))
        else:
            pieces.append(wide[at * outs : (at + 1) * outs, :])

    def piece(depth, tap):
        return pieces[depth * 9 + tap]

    for tap in range(9):
        for plane in range(4):
            block = jnp.zeros((outs, 128), F32)
            for depth in range(3):
                block = jnp.where(group == plane + depth - 1, piece(depth, tap), block)
            own[plane * outs : (plane + 1) * outs, tap * 128 : (tap + 1) * 128] = block.astype(BF)
    for dst, depth in ((low, 0), (high, 2)):
        for part in range(3):
            block = jnp.zeros((outs, 128), F32)
            for lane in range(4):
                if part * 4 + lane < 9:
                    block = jnp.where(group == lane, piece(depth, part * 4 + lane), block)
            dst[:, part * 128 : (part + 1) * 128] = block.astype(BF)


def kernel(
    count, batches, vol_hbm, w1_hbm, w2_hbm, w3_hbm, dw_ref, out_ref,
    vol_ref, w1_ref, w2_ref, w3_ref, pick, pick_last,
    own1, low1, high1, own2, low2, high2, own3, low3, high3,
    x_ref, vh, h1, hh, xcol, hcol, acc, sent, slab, edge, xcol3, hcol3, wd, fin,
    v_send, v_recv, h_send, h_recv, p_send, p_recv, e_send, e_recv,
    w_send, w_recv, f_send, f_recv, load_sem,
):
    me = lax.axis_index("space")
    lot = lax.axis_index("batch")
    parity = lax.rem(me, 2)
    block = me // 2
    blocks = count // 2
    right = lax.rem(me + 1, count)
    left = lax.rem(me + count - 1, count)
    shards = batches // blocks

    def own_part(values, weight, sample):
        put_taps(values, xcol, 0, NXY)
        for part in range(4):
            cols = slice(part * 256, (part + 1) * 256)
            acc[sample, :, cols] = dot(weight[...], xcol[:, cols])

    gives = lot // shards == block
    barrier = pltpu.get_barrier_semaphore()
    for step in range(1, count):
        pl.semaphore_signal(
            barrier, inc=1, device_id={"space": lax.rem(me + step, count)}, device_id_type=MESH
        )
    for slot in range(shards):
        owner = block * shards + slot

        @pl.when(owner != lot)
        def _():
            pl.semaphore_signal(barrier, inc=1, device_id={"batch": owner}, device_id_type=MESH)

    loads = [
        pltpu.make_async_copy(src, dst, load_sem.at[at])
        for at, (src, dst) in enumerate(
            ((w1_hbm, w1_ref), (vol_hbm, vol_ref), (w2_hbm, w2_ref), (w3_hbm, w3_ref))
        )
    ]
    for load in loads:
        load.start()

    half = NXY // 2
    at = lax.broadcasted_iota(jnp.int32, (NXY * NXY, half * half), 0)
    cell = lax.broadcasted_iota(jnp.int32, (NXY * NXY, half * half), 1)
    pick[...] = jnp.where(at == (cell // half) * 2 * NXY + (cell % half) * 2, 1.0, 0.0).astype(BF)
    spot = lax.broadcasted_iota(jnp.int32, (half * half, 1024), 0)
    feat = lax.broadcasted_iota(jnp.int32, (half * half, 1024), 1) % 16
    pick_last[...] = jnp.where(
        spot == (feat // 4) * 4 * half + (feat % 4) * 4, 1.0, 0.0
    ).astype(BF)
    order = (parity, 1 - parity)
    loads[0].wait()
    lay_weights(w1_ref, own1, low1, high1, C1)
    loads[1].wait()
    for sample in range(2):
        for plane in range(4):
            x_ref[sample, plane * C1 : (plane + 1) * C1, :] = vol_ref[sample, :, plane, :]
    own_part(x_ref[parity], own1, parity)
    own_part(x_ref[1 - parity], own1, 1 - parity)
    @pl.when(gives)
    def _():
        pl.semaphore_wait(barrier, count + batches - 2)

    @pl.when(jnp.logical_not(gives))
    def _():
        pl.semaphore_wait(barrier, count - 1)

    def halo_copies(src, dst, send, recv, sample):
        up = pltpu.make_async_remote_copy(
            src_ref=src.at[sample, 96:128], dst_ref=dst.at[sample, 0],
            send_sem=send.at[sample, 0], recv_sem=recv.at[sample, 0],
            device_id={"space": right}, device_id_type=MESH,
        )
        down = pltpu.make_async_remote_copy(
            src_ref=src.at[sample, 0:32], dst_ref=dst.at[sample, 1],
            send_sem=send.at[sample, 1], recv_sem=recv.at[sample, 1],
            device_id={"space": left}, device_id_type=MESH,
        )
        return up, down

    v_copies = [halo_copies(x_ref, vh, v_send, v_recv, sample) for sample in order]
    for pair in v_copies:
        for copy in pair:
            copy.start()

    def row_copy(step):
        target = lax.rem(lot + step, batches)
        return pltpu.make_async_remote_copy(
            src_ref=dw_ref, dst_ref=wd.at[lax.rem(lot, shards)],
            send_sem=w_send.at[step], recv_sem=w_recv.at[lax.rem(lot, shards)],
            device_id={"batch": target}, device_id_type=MESH,
        )

    own_rows = pltpu.make_async_copy(dw_ref, wd.at[lax.rem(lot, shards)], load_sem.at[4])

    @pl.when(gives)
    def _():
        for step in range(1, batches):
            row_copy(step).start()
        own_rows.start()


    def halo_part(halo, low, high, sample):
        put_taps(halo[sample, 0], hcol, 0, NXY)
        put_taps(halo[sample, 1], hcol, 288, NXY)
        for part in range(4):
            cols = slice(part * 256, (part + 1) * 256)
            acc[sample, 0:32, cols] += dot(low[:, 0:288], hcol[0:288, cols])
            acc[sample, 96:128, cols] += dot(high[:, 0:288], hcol[288:576, cols])

    for sample in order[2:]:
        own_part(x_ref[sample], own1, sample)
    loads[2].wait()
    lay_weights(w2_ref, own2, low2, high2, C1)
    loads[3].wait()
    lay_weights(w3_ref, own3, low3, high3, 2 * C1)
    h_copies = []
    for sample, pair in zip(order, v_copies):
        for copy in pair:
            copy.wait_recv()
        halo_part(vh, low1, high1, sample)
        h1[sample] = activate(acc[sample]).astype(BF)
        pair = halo_copies(h1, hh, h_send, h_recv, sample)
        for copy in pair:
            copy.start()
        h_copies.append(pair)

    def pooled_of(sample):
        low = jnp.maximum(acc[sample, 0:32], acc[sample, 32:64])
        high = jnp.maximum(acc[sample, 64:96], acc[sample, 96:128])
        best = jnp.concatenate([low, high], axis=0)
        best = jnp.maximum(best, ahead(best, 1))
        best = jnp.maximum(best, ahead(best, NXY))
        return dot(activate(best).astype(BF), pick[...]).astype(BF)

    def edge_copy(src, owner, slot):
        step = jnp.where(parity == 0, blocks - 1, 1)
        target = lax.rem(block + step, blocks) * 2 + owner
        return pltpu.make_async_remote_copy(
            src_ref=src.at[pl.ds(pl.multiple_of(parity * C1, C1), C1)],
            dst_ref=edge.at[1 - parity],
            send_sem=e_send.at[slot], recv_sem=e_recv.at[1 - parity],
            device_id={"space": target}, device_id_type=MESH,
        )

    partner_copy = pltpu.make_async_remote_copy(
        src_ref=sent, dst_ref=slab.at[parity], send_sem=p_send, recv_sem=p_recv,
        device_id={"space": block * 2 + 1 - parity}, device_id_type=MESH,
    )
    edge_copies = (edge_copy(sent, 1 - parity, 0), edge_copy(slab.at[parity], parity, 1))
    for turn in (1, 0):
        sample = order[turn]
        put = h1[sample]
        own_part(put, own2, sample)
        for copy in h_copies[turn]:
            copy.wait_recv()
        halo_part(hh, low2, high2, sample)
        pooled = pooled_of(sample)
        if turn == 1:
            sent[...] = pooled
            edge_copies[0].start()
            partner_copy.start()
        else:
            slab[parity] = pooled
            edge_copies[1].start()

    partner_copy.wait_recv()
    put_taps(jnp.concatenate([slab[0], slab[1]], axis=0), xcol3, 0, half)
    third = dot(own3[...], xcol3[...])
    for side in range(2):
        pltpu.make_async_remote_copy(
            src_ref=edge.at[side], dst_ref=edge.at[side],
            send_sem=e_send.at[side], recv_sem=e_recv.at[side],
            device_id={"space": right}, device_id_type=MESH,
        ).wait_recv()
    put_taps(edge[0], hcol3, 0, half)
    put_taps(edge[1], hcol3, 288, half)
    outs = 2 * C1
    best = jnp.maximum(
        jnp.maximum(third[outs : 2 * outs], third[2 * outs : 3 * outs]),
        jnp.maximum(
            third[0:outs] + dot(low3[:, 0:288], hcol3[0:288, :]),
            third[3 * outs :] + dot(high3[:, 0:288], hcol3[288:576, :]),
        ),
    )
    for off in (1, 2, half, 2 * half):
        best = jnp.maximum(best, ahead(best, off))
    cells = dot(activate(best).astype(BF), pick_last[...])
    mine = lax.broadcasted_iota(jnp.int32, cells.shape, 1) // 16
    mine = mine == lax.broadcasted_iota(jnp.int32, cells.shape, 0)
    feats = jnp.sum(jnp.where(mine, cells, 0.0), axis=0, keepdims=True).astype(BF)
    for slot in range(shards):
        @pl.when(block * shards + slot != lot)
        def _():
            pltpu.make_async_remote_copy(
                src_ref=dw_ref, dst_ref=wd.at[slot],
                send_sem=w_send.at[0], recv_sem=w_recv.at[slot],
                device_id={"batch": lax.rem(lot + 1, batches)}, device_id_type=MESH,
            ).wait_recv()

    @pl.when(gives)
    def _():
        own_rows.wait()

    rows = dw_ref.shape[0]
    total = jnp.zeros((8, 128), F32)
    feats = jnp.broadcast_to(feats.astype(F32), (8, feats.shape[1])).astype(BF)
    for slot in range(shards):
        total += dot(feats[:, slot * rows : (slot + 1) * rows], wd[slot])
    fin[me] = total

    def fin_copy(step):
        return pltpu.make_async_remote_copy(
            src_ref=fin.at[me], dst_ref=fin.at[me],
            send_sem=f_send.at[step], recv_sem=f_recv.at[step],
            device_id={"space": lax.rem(me + step, count)}, device_id_type=MESH,
        )

    fin_copies = [fin_copy(step) for step in range(1, count)]
    for copy in fin_copies:
        copy.start()
    for pair in v_copies + h_copies:
        for copy in pair:
            copy.wait_send()
    for copy in edge_copies:
        copy.wait_send()
    partner_copy.wait_send()

    @pl.when(gives)
    def _():
        for step in range(1, batches):
            row_copy(step).wait_send()

    for copy in fin_copies:
        copy.wait_send()
    for step in range(1, count):
        source = lax.rem(me + count - step, count)
        pltpu.make_async_remote_copy(
            src_ref=fin.at[source], dst_ref=fin.at[source],
            send_sem=f_send.at[step], recv_sem=f_recv.at[step],
            device_id={"space": right}, device_id_type=MESH,
        ).wait_recv()
    for sample in range(2):
        row = fin[sample]
        for other in range(1, blocks):
            row = row + fin[2 * other + sample]
        out_ref[sample : sample + 1, :] = row[0:1, :]


def per_device(count, batches, volume, conv_one, conv_two, conv_three, dense_weight):
    flat = NXY * NXY
    small = flat // 4
    shards = batches // (count // 2)
    vmem, dma = pltpu.VMEM, pltpu.SemaphoreType.DMA
    return pl.pallas_call(
        functools.partial(kernel, count, batches),
        out_shape=jax.ShapeDtypeStruct((2, dense_weight.shape[1]), F32),
        in_specs=[pl.BlockSpec(memory_space=pltpu.HBM)] * 5,
        out_specs=pl.BlockSpec(memory_space=vmem),
        scratch_shapes=[
            vmem(volume.shape, BF), vmem((864, C1), BF), vmem((864, C1), BF),
            vmem((864, 2 * C1), BF), vmem((flat, small), BF), vmem((small, 1024), BF),
            vmem((128, 1152), BF), vmem((32, 384), BF), vmem((32, 384), BF),
            vmem((128, 1152), BF), vmem((32, 384), BF), vmem((32, 384), BF),
            vmem((256, 1152), BF), vmem((64, 384), BF), vmem((64, 384), BF),
            vmem((2, 128, flat), BF),
            vmem((2, 2, 32, flat), BF),
            vmem((2, 128, flat), BF),
            vmem((2, 2, 32, flat), BF),
            vmem((1152, flat), BF),
            vmem((576, flat), BF),
            vmem((2, 128, flat), F32),
            vmem((64, small), BF),
            vmem((2, 64, small), BF),
            vmem((2, 32, small), BF),
            vmem((1152, small), BF),
            vmem((576, small), BF),
            vmem((shards,) + dense_weight.shape, BF),
            vmem((count, 8, 128), F32),
            dma((2, 2)), dma((2, 2)), dma((2, 2)), dma((2, 2)),
            dma, dma, dma((2,)), dma((2,)),
            dma((batches,)), dma((shards,)), dma((count,)), dma((count,)), dma((5,)),
        ],
        compiler_params=pltpu.CompilerParams(
            collective_id=0, has_side_effects=True, vmem_limit_bytes=60 << 20
        ),
    )(
        volume,
        conv_one.reshape(-1, C1),
        conv_two.reshape(-1, C1),
        jnp.swapaxes(conv_three, 3, 4).reshape(-1, 2 * C1),
        dense_weight,
    )


def solution(mesh):
    in_specs = (P("batch", None, "space", None), P(), P(), P(), P("batch", None))
    return jax.shard_map(
        functools.partial(per_device, mesh.shape["space"], mesh.shape["batch"]),
        mesh=mesh,
        in_specs=in_specs,
        out_specs=P("batch", None),
        check_vma=False,
    )
```

```python
import functools

import jax
import jax.numpy as jnp
from jax import lax
from jax.experimental import pallas as pl
from jax.experimental.pallas import tpu as pltpu
from jax.sharding import PartitionSpec as P

NXY = 32
C1 = 32
BF = jnp.bfloat16
F32 = jnp.float32
MESH = pl.DeviceIdType.MESH


def activate(values):
    return jnp.where(values > 0, values, 0.3 * values)


def dot(lhs, rhs):
    return jnp.dot(lhs, rhs, preferred_element_type=F32)


def ahead(values, off):
    return pltpu.roll(values, (-off) % values.shape[1], 1)


def put_taps(values, dst, base, extent):
    rows = values.shape[0]
    column = lax.broadcasted_iota(jnp.int32, values.shape, 1) % extent
    for col_idx in range(3):
        off = col_idx - 1
        moved = values
        if off:
            border = extent - 1 if off == 1 else 0
            moved = jnp.where(
                column == border, ahead(values, off - off * extent), ahead(values, off)
            )
        for row_idx in range(3):
            tap = row_idx * 3 + col_idx
            turned = ahead(moved, (row_idx - 1) * extent) if row_idx != 1 else moved
            dst[base + tap * rows : base + (tap + 1) * rows, :] = turned


def lay_weights(w_ref, own, low, high, outs):
    spread = (
        lax.broadcasted_iota(jnp.int32, (C1, 128), 1) % C1
        == lax.broadcasted_iota(jnp.int32, (C1, 128), 0)
    )
    spread = jnp.where(spread, 1.0, 0.0).astype(BF)
    turned = w_ref.shape[1] != C1
    wide = w_ref[...].T if turned else dot(w_ref[...], spread)
    group = lax.broadcasted_iota(jnp.int32, (outs, 128), 1) // C1

    pieces = []
    for at in range(27):
        if turned:
            pieces.append(dot(wide[:, at * C1 : (at + 1) * C1], spread))
        else:
            pieces.append(wide[at * outs : (at + 1) * outs, :])

    def piece(depth, tap):
        return pieces[depth * 9 + tap]

    for tap in range(9):
        for plane in range(4):
            block = jnp.zeros((outs, 128), F32)
            for depth in range(3):
                block = jnp.where(group == plane + depth - 1, piece(depth, tap), block)
            own[plane * outs : (plane + 1) * outs, tap * 128 : (tap + 1) * 128] = block.astype(BF)
    for dst, depth in ((low, 0), (high, 2)):
        for part in range(3):
            block = jnp.zeros((outs, 128), F32)
            for lane in range(4):
                if part * 4 + lane < 9:
                    block = jnp.where(group == lane, piece(depth, part * 4 + lane), block)
            dst[:, part * 128 : (part + 1) * 128] = block.astype(BF)


def kernel(
    count, batches, vol_hbm, w1_hbm, w2_hbm, w3_hbm, dw_ref, out_ref,
    vol_ref, w1_ref, w2_ref, w3_ref, pick, pick_last,
    own1, low1, high1, own2, low2, high2, own3, low3, high3,
    x_ref, vh, h1, hh, xcol, hcol, acc, sent, slab, edge, xcol3, hcol3, wd, fin,
    v_send, v_recv, h_send, h_recv, p_send, p_recv, e_send, e_recv,
    w_send, w_recv, f_send, f_recv, load_sem,
):
    me = lax.axis_index("space")
    lot = lax.axis_index("batch")
    parity = lax.rem(me, 2)
    block = me // 2
    blocks = count // 2
    right = lax.rem(me + 1, count)
    left = lax.rem(me + count - 1, count)
    shards = batches // blocks

    def own_part(values, weight, sample):
        put_taps(values, xcol, 0, NXY)
        for part in range(4):
            cols = slice(part * 256, (part + 1) * 256)
            acc[sample, :, cols] = dot(weight[...], xcol[:, cols])

    gives = lot // shards == block
    barrier = pltpu.get_barrier_semaphore()
    for slot in range(shards):
        owner = block * shards + slot

        @pl.when(owner != lot)
        def _():
            pl.semaphore_signal(barrier, inc=1, device_id={"batch": owner}, device_id_type=MESH)

    for step in range(1, count):
        pl.semaphore_signal(
            barrier, inc=1, device_id={"space": lax.rem(me + step, count)}, device_id_type=MESH
        )

    loads = [
        pltpu.make_async_copy(src, dst, load_sem.at[at])
        for at, (src, dst) in enumerate(
            ((w1_hbm, w1_ref), (vol_hbm, vol_ref), (w2_hbm, w2_ref), (w3_hbm, w3_ref))
        )
    ]
    for load in loads:
        load.start()

    half = NXY // 2
    at = lax.broadcasted_iota(jnp.int32, (NXY * NXY, half * half), 0)
    cell = lax.broadcasted_iota(jnp.int32, (NXY * NXY, half * half), 1)
    pick[...] = jnp.where(at == (cell // half) * 2 * NXY + (cell % half) * 2, 1.0, 0.0).astype(BF)
    spot = lax.broadcasted_iota(jnp.int32, (half * half, 1024), 0)
    feat = lax.broadcasted_iota(jnp.int32, (half * half, 1024), 1) % 16
    pick_last[...] = jnp.where(
        spot == (feat // 4) * 4 * half + (feat % 4) * 4, 1.0, 0.0
    ).astype(BF)
    order = (parity, 1 - parity)
    loads[0].wait()
    lay_weights(w1_ref, own1, low1, high1, C1)
    loads[1].wait()
    for sample in range(2):
        for plane in range(4):
            x_ref[sample, plane * C1 : (plane + 1) * C1, :] = vol_ref[sample, :, plane, :]
    own_part(x_ref[parity], own1, parity)
    own_part(x_ref[1 - parity], own1, 1 - parity)
    @pl.when(gives)
    def _():
        pl.semaphore_wait(barrier, count + batches - 2)

    @pl.when(jnp.logical_not(gives))
    def _():
        pl.semaphore_wait(barrier, count - 1)

    def halo_copies(src, dst, send, recv, sample):
        up = pltpu.make_async_remote_copy(
            src_ref=src.at[sample, 96:128], dst_ref=dst.at[sample, 0],
            send_sem=send.at[sample, 0], recv_sem=recv.at[sample, 0],
            device_id={"space": right}, device_id_type=MESH,
        )
        down = pltpu.make_async_remote_copy(
            src_ref=src.at[sample, 0:32], dst_ref=dst.at[sample, 1],
            send_sem=send.at[sample, 1], recv_sem=recv.at[sample, 1],
            device_id={"space": left}, device_id_type=MESH,
        )
        return up, down

    v_copies = [halo_copies(x_ref, vh, v_send, v_recv, sample) for sample in order]
    for pair in v_copies:
        for copy in pair:
            copy.start()

    def row_copy(step):
        target = lax.rem(lot + step, batches)
        return pltpu.make_async_remote_copy(
            src_ref=dw_ref, dst_ref=wd.at[lax.rem(lot, shards)],
            send_sem=w_send.at[step], recv_sem=w_recv.at[lax.rem(lot, shards)],
            device_id={"batch": target}, device_id_type=MESH,
        )

    own_rows = pltpu.make_async_copy(dw_ref, wd.at[lax.rem(lot, shards)], load_sem.at[4])

    @pl.when(gives)
    def _():
        for step in sorted(range(1, batches), key=lambda n: -min(n, batches - n)):
            row_copy(step).start()
        own_rows.start()


    def halo_part(halo, low, high, sample):
        put_taps(halo[sample, 0], hcol, 0, NXY)
        put_taps(halo[sample, 1], hcol, 288, NXY)
        for part in range(4):
            cols = slice(part * 256, (part + 1) * 256)
            acc[sample, 0:32, cols] += dot(low[:, 0:288], hcol[0:288, cols])
            acc[sample, 96:128, cols] += dot(high[:, 0:288], hcol[288:576, cols])

    for sample in order[2:]:
        own_part(x_ref[sample], own1, sample)
    loads[2].wait()
    lay_weights(w2_ref, own2, low2, high2, C1)
    loads[3].wait()
    lay_weights(w3_ref, own3, low3, high3, 2 * C1)
    h_copies = []
    for sample, pair in zip(order, v_copies):
        for copy in pair:
            copy.wait_recv()
        halo_part(vh, low1, high1, sample)
        h1[sample] = activate(acc[sample]).astype(BF)
        pair = halo_copies(h1, hh, h_send, h_recv, sample)
        for copy in pair:
            copy.start()
        h_copies.append(pair)

    def pooled_of(sample):
        low = jnp.maximum(acc[sample, 0:32], acc[sample, 32:64])
        high = jnp.maximum(acc[sample, 64:96], acc[sample, 96:128])
        best = jnp.concatenate([low, high], axis=0)
        best = jnp.maximum(best, ahead(best, 1))
        best = jnp.maximum(best, ahead(best, NXY))
        return dot(activate(best).astype(BF), pick[...]).astype(BF)

    def edge_copy(src, owner, slot):
        step = jnp.where(parity == 0, blocks - 1, 1)
        target = lax.rem(block + step, blocks) * 2 + owner
        return pltpu.make_async_remote_copy(
            src_ref=src.at[pl.ds(pl.multiple_of(parity * C1, C1), C1)],
            dst_ref=edge.at[1 - parity],
            send_sem=e_send.at[slot], recv_sem=e_recv.at[1 - parity],
            device_id={"space": target}, device_id_type=MESH,
        )

    partner_copy = pltpu.make_async_remote_copy(
        src_ref=sent, dst_ref=slab.at[parity], send_sem=p_send, recv_sem=p_recv,
        device_id={"space": block * 2 + 1 - parity}, device_id_type=MESH,
    )
    edge_copies = (edge_copy(sent, 1 - parity, 0), edge_copy(slab.at[parity], parity, 1))
    for turn in (1, 0):
        sample = order[turn]
        put = h1[sample]
        own_part(put, own2, sample)
        for copy in h_copies[turn]:
            copy.wait_recv()
        halo_part(hh, low2, high2, sample)
        pooled = pooled_of(sample)
        if turn == 1:
            sent[...] = pooled
            edge_copies[0].start()
            partner_copy.start()
        else:
            slab[parity] = pooled
            edge_copies[1].start()

    partner_copy.wait_recv()
    put_taps(jnp.concatenate([slab[0], slab[1]], axis=0), xcol3, 0, half)
    third = dot(own3[...], xcol3[...])
    for side in range(2):
        pltpu.make_async_remote_copy(
            src_ref=edge.at[side], dst_ref=edge.at[side],
            send_sem=e_send.at[side], recv_sem=e_recv.at[side],
            device_id={"space": right}, device_id_type=MESH,
        ).wait_recv()
    put_taps(edge[0], hcol3, 0, half)
    put_taps(edge[1], hcol3, 288, half)
    outs = 2 * C1
    best = jnp.maximum(
        jnp.maximum(third[outs : 2 * outs], third[2 * outs : 3 * outs]),
        jnp.maximum(
            third[0:outs] + dot(low3[:, 0:288], hcol3[0:288, :]),
            third[3 * outs :] + dot(high3[:, 0:288], hcol3[288:576, :]),
        ),
    )
    for off in (1, 2, half, 2 * half):
        best = jnp.maximum(best, ahead(best, off))
    cells = dot(activate(best).astype(BF), pick_last[...])
    mine = lax.broadcasted_iota(jnp.int32, cells.shape, 1) // 16
    mine = mine == lax.broadcasted_iota(jnp.int32, cells.shape, 0)
    feats = jnp.sum(jnp.where(mine, cells, 0.0), axis=0, keepdims=True).astype(BF)
    for slot in range(shards):
        @pl.when(block * shards + slot != lot)
        def _():
            pltpu.make_async_remote_copy(
                src_ref=dw_ref, dst_ref=wd.at[slot],
                send_sem=w_send.at[0], recv_sem=w_recv.at[slot],
                device_id={"batch": lax.rem(lot + 1, batches)}, device_id_type=MESH,
            ).wait_recv()

    @pl.when(gives)
    def _():
        own_rows.wait()

    rows = dw_ref.shape[0]
    total = jnp.zeros((8, 128), F32)
    feats = jnp.broadcast_to(feats.astype(F32), (8, feats.shape[1])).astype(BF)
    for slot in range(shards):
        total += dot(feats[:, slot * rows : (slot + 1) * rows], wd[slot])
    fin[me] = total

    def fin_copy(step):
        return pltpu.make_async_remote_copy(
            src_ref=fin.at[me], dst_ref=fin.at[me],
            send_sem=f_send.at[step], recv_sem=f_recv.at[step],
            device_id={"space": lax.rem(me + step, count)}, device_id_type=MESH,
        )

    fin_copies = [fin_copy(step) for step in range(1, count)]
    for copy in fin_copies:
        copy.start()
    for pair in v_copies + h_copies:
        for copy in pair:
            copy.wait_send()
    for copy in edge_copies:
        copy.wait_send()
    partner_copy.wait_send()

    @pl.when(gives)
    def _():
        for step in range(1, batches):
            row_copy(step).wait_send()

    for copy in fin_copies:
        copy.wait_send()
    for step in range(1, count):
        source = lax.rem(me + count - step, count)
        pltpu.make_async_remote_copy(
            src_ref=fin.at[source], dst_ref=fin.at[source],
            send_sem=f_send.at[step], recv_sem=f_recv.at[step],
            device_id={"space": right}, device_id_type=MESH,
        ).wait_recv()
    for sample in range(2):
        row = fin[sample]
        for other in range(1, blocks):
            row = row + fin[2 * other + sample]
        out_ref[sample : sample + 1, :] = row[0:1, :]


def per_device(count, batches, volume, conv_one, conv_two, conv_three, dense_weight):
    flat = NXY * NXY
    small = flat // 4
    shards = batches // (count // 2)
    vmem, dma = pltpu.VMEM, pltpu.SemaphoreType.DMA
    return pl.pallas_call(
        functools.partial(kernel, count, batches),
        out_shape=jax.ShapeDtypeStruct((2, dense_weight.shape[1]), F32),
        in_specs=[pl.BlockSpec(memory_space=pltpu.HBM)] * 5,
        out_specs=pl.BlockSpec(memory_space=vmem),
        scratch_shapes=[
            vmem(volume.shape, BF), vmem((864, C1), BF), vmem((864, C1), BF),
            vmem((864, 2 * C1), BF), vmem((flat, small), BF), vmem((small, 1024), BF),
            vmem((128, 1152), BF), vmem((32, 384), BF), vmem((32, 384), BF),
            vmem((128, 1152), BF), vmem((32, 384), BF), vmem((32, 384), BF),
            vmem((256, 1152), BF), vmem((64, 384), BF), vmem((64, 384), BF),
            vmem((2, 128, flat), BF),
            vmem((2, 2, 32, flat), BF),
            vmem((2, 128, flat), BF),
            vmem((2, 2, 32, flat), BF),
            vmem((1152, flat), BF),
            vmem((576, flat), BF),
            vmem((2, 128, flat), F32),
            vmem((64, small), BF),
            vmem((2, 64, small), BF),
            vmem((2, 32, small), BF),
            vmem((1152, small), BF),
            vmem((576, small), BF),
            vmem((shards,) + dense_weight.shape, BF),
            vmem((count, 8, 128), F32),
            dma((2, 2)), dma((2, 2)), dma((2, 2)), dma((2, 2)),
            dma, dma, dma((2,)), dma((2,)),
            dma((batches,)), dma((shards,)), dma((count,)), dma((count,)), dma((5,)),
        ],
        compiler_params=pltpu.CompilerParams(
            collective_id=0, has_side_effects=True, vmem_limit_bytes=60 << 20
        ),
    )(
        volume,
        conv_one.reshape(-1, C1),
        conv_two.reshape(-1, C1),
        jnp.swapaxes(conv_three, 3, 4).reshape(-1, 2 * C1),
        dense_weight,
    )


def solution(mesh):
    in_specs = (P("batch", None, "space", None), P(), P(), P(), P("batch", None))
    return jax.shard_map(
        functools.partial(per_device, mesh.shape["space"], mesh.shape["batch"]),
        mesh=mesh,
        in_specs=in_specs,
        out_specs=P("batch", None),
        check_vma=False,
    )
```
